32 devices in a mesh: site: 4 (over y, x), sector: 8 (over z, core).
Axes of the slice: x: 2, y: 2, z: 4, core: 2. Of those that a mesh axis runs over, the one named last changes fastest.
Arguments:
- boundary: bfloat16 [4, 2048, 32, 256], P('site', 'sector'), may hold values from -0.375 to 0.375
- peps_row: bfloat16 [4, 32, 8], P('site'), may hold values from -1 to 1
- sketch: bfloat16 [4, 2048, 8, 256], P('site', 'sector'), may hold values from -0.125 to 0.125
- charges: int32 [4, 8], P('site'), may hold values from -1 to 1
- left_edge: bfloat16 [512, 2048], P(None, 'sector'), may hold values from -6 to 6
Outputs:
- environments: float32 [4, 512, 2048], P('site', None, 'sector')
The draws below stay inside these ranges and needn't reach their ends.
Inputs may be any that keep to these rules, and one draw needn't show every extreme that they name: `charges`: each entry is a charge change of -1, 0 or +1.
All inputs are finite; a program needn't handle non-finite values.
Results may differ from the reference program's by a relative error of at most 0.0003.
Values sent between devices are 32-bit elements; how exact they have to be, the bound alone decides.
A program may use at most 64 MiB of HBM per device.

```python
import jax
import jax.numpy as jnp
from jax import lax

W = 256
P_SIZE = 32
D = 8
ROWS = 512
SITES = 4
CHI = 2048
N_SECTOR = 8


def place_ends(values, own_key, least, high):
    shape = values.shape
    spot = [jax.random.randint(jax.random.fold_in(own_key, axis), (), 0, shape[axis]) for axis in range(len(shape))]
    values = values.at[tuple(spot)].set(least)
    longest = shape.index(max(shape))
    spot[longest] = (spot[longest] + 1) % shape[longest]
    return values.at[tuple(spot)].set(high)


def level_of(stream_key, extent, pieces, low, top_value):
    level, own = 1.0, jax.random.fold_in(stream_key, 6)
    for axis_at, blocks in pieces:
        heights = jnp.exp(jax.random.uniform(jax.random.fold_in(own, axis_at), (blocks,), jnp.float32, low / len(pieces), top_value / len(pieces)))
        level = level * jnp.repeat(heights, extent[axis_at] // blocks).reshape([-1 if axis == axis_at else 1 for axis in range(len(extent))])
    return level


def centred(own_key, extent, scale, bound, split=(), held_as=jnp.bfloat16):
    level = level_of(own_key, extent, split, -0.22, 0.18) if split else 1.0
    entries = jax.random.normal(own_key, extent, jnp.float32) * scale * level
    return jnp.minimum(jnp.maximum(entries, -bound), bound).astype(held_as)


def setup_inputs(seed: int = 0) -> dict:
    key_of = jax.random.split(jax.random.key(seed), 6)
    return {
        "boundary": centred(key_of[0], (SITES, CHI, P_SIZE, W), W ** -0.5, 0.375, ((0, 4), (1, 8))),
        "peps_row": centred(key_of[1], (SITES, P_SIZE, D), P_SIZE ** -0.5, 1.0, ((0, 4),)),
        "sketch": centred(key_of[2], (SITES, CHI, D, W), (W * D) ** -0.5, 0.125, ((0, 4), (1, 8))),
        "charges": place_ends(jax.random.randint(key_of[3], (SITES, D), -1, 2), jax.random.fold_in(key_of[3], 1), -1, 1).astype(jnp.int32),
        "left_edge": centred(key_of[4], (ROWS, CHI), 1.0, 6.0, ((1, 8),)),
    }


def reference(boundary, peps_row, sketch, charges, left_edge):
    absorbed = jnp.einsum('jipv,jpl->jilv', boundary.astype(jnp.float32), peps_row.astype(jnp.float32), precision=lax.Precision.HIGHEST)

    def absorb_site(state_rows, inputs):
        block_tensor, block_sketch, charge_row = inputs
        block_tensor = block_tensor.reshape(N_SECTOR, W, D, W)
        block_sketch = block_sketch.astype(jnp.float32).reshape(N_SECTOR, W, D, W)
        onehot = (charge_row[:, None] == jnp.arange(-1, 2, dtype=jnp.int32)[None, :]).astype(jnp.float32)
        transfer = jnp.einsum('bwlv,bvlu,ls->bswu', block_tensor, block_sketch, onehot, precision=lax.Precision.HIGHEST)
        blocked = state_rows.reshape(ROWS, N_SECTOR, W)
        parts = jnp.einsum('rbw,bswu->srbu', blocked, transfer, precision=lax.Precision.HIGHEST)
        empty_rows = jnp.zeros((ROWS, 1, W), jnp.float32)
        updated = parts[1] + jnp.concatenate([empty_rows, parts[2][:, :-1]], axis=1) + jnp.concatenate([parts[0][:, 1:], empty_rows], axis=1)
        updated = updated.reshape(ROWS, N_SECTOR * W)
        return updated, updated

    start_rows = left_edge.astype(jnp.float32)
    final_rows, environments = lax.scan(absorb_site, start_rows, (absorbed, sketch, charges))
    return environments
```

```python
import functools

import jax
import jax.numpy as jnp
from jax import lax
from jax.experimental import pallas as pl
from jax.experimental.pallas import tpu as pltpu
from jax.sharding import PartitionSpec as P

MESH = pl.DeviceIdType.MESH
CHUNK_ROWS = 64
LAG = 1
MAP_ROWS = 64


def dot(a, b):
    return jnp.dot(a, b, preferred_element_type=jnp.float32)


def split(x):
    high = x.astype(jnp.bfloat16)
    low = (x - high.astype(jnp.float32)).astype(jnp.bfloat16)
    return high, low


def kernel(
    sites,
    sectors,
    width,
    phys,
    depth,
    boundary_ref,
    peps_ref,
    sketch_ref,
    charges_ref,
    left_ref,
    out_ref,
    boundary,
    sketch,
    absorbed,
    sorted_sketch,
    map_high,
    map_low,
    state,
    from_below,
    from_above,
    upward,
    downward,
    boundary_sem,
    sketch_sem,
    state_send,
    state_recv,
    up_send,
    up_recv,
    down_send,
    down_recv,
):
    site = lax.axis_index("site")
    sector = lax.axis_index("sector")
    rows = left_ref.shape[0]
    chunks = rows // CHUNK_ROWS
    steps = width // MAP_ROWS
    f32, bf16 = jnp.float32, jnp.bfloat16

    sketch_copy = pltpu.make_async_copy(sketch_ref, sketch, sketch_sem)
    sketch_copy.start()
    slab = MAP_ROWS * phys
    slabs = []
    for i in range(steps):
        part = pl.ds(i * slab, slab)
        copy = pltpu.make_async_copy(boundary_ref.at[part], boundary.at[part], boundary_sem.at[i])
        copy.start()
        slabs.append(copy)

    barrier = pltpu.get_barrier_semaphore()
    has_prev, has_next = site > 0, site < sites - 1
    has_below, has_above = sector > 0, sector < sectors - 1

    def greet(condition, target):
        @pl.when(condition)
        def _():
            pl.semaphore_signal(barrier, inc=1, device_id=target, device_id_type=MESH)

    prev_id, next_id = (site - 1, sector), (site + 1, sector)
    below_id, above_id = (site, sector - 1), (site, sector + 1)
    greet(has_prev, prev_id)
    greet(has_next, next_id)
    greet(has_below, below_id)
    greet(has_above, above_id)

    @pl.when(site == 0)
    def _():
        state[...] = left_ref[...].astype(f32)

    group = width // phys
    size = group * depth
    iota = lambda shape, axis: lax.broadcasted_iota(jnp.int32, shape, axis)
    pick = (iota((size, depth), 0) // group == iota((size, depth), 1)).astype(f32).astype(bf16)
    tile = (iota((phys, width), 1) % phys == iota((phys, width), 0)).astype(f32).astype(bf16)
    by_row = dot(pick, peps_ref[...]).astype(bf16)
    same = iota((size, width), 0) % group == iota((size, width), 1) // phys
    spread = jnp.where(same, dot(by_row, tile), 0.0).astype(bf16)

    run = width // depth
    order = (
        iota((width, width), 1) == (iota((width, width), 0) % run) * depth + iota((width, width), 0) // run
    ).astype(f32).astype(bf16)
    sketch_copy.wait()
    for g in range(depth):
        moved = dot(order, sketch[pl.ds(g * width, width), :]).astype(bf16)
        for l in range(depth):
            sorted_sketch[l, pl.ds(g * run, run), :] = moved[l * run : (l + 1) * run]

    flags = [
        [(charges_ref[0, l] == s - 1).astype(f32) for l in range(depth)] for s in range(3)
    ]
    for i in range(steps):
        slabs[i].wait()
        for g in range(MAP_ROWS // group):
            start = (i * MAP_ROWS + g * group) * phys
            grown = dot(spread, boundary[pl.ds(start, width), :])
            for l in range(depth):
                absorbed[l, pl.ds(g * group, group), :] = grown[l * group : (l + 1) * group]
        sums = [None] * 3
        for l in range(depth):
            high, low = split(absorbed[l])
            block = sorted_sketch[l]
            product = dot(high, block) + dot(low, block)
            for s in range(3):
                term = flags[s][l] * product
                sums[s] = term if sums[s] is None else sums[s] + term
        for s in range(3):
            high, low = split(sums[s])
            map_high[pl.ds(i * MAP_ROWS, MAP_ROWS), pl.ds(s * width, width)] = high
            map_low[pl.ds(i * MAP_ROWS, MAP_ROWS), pl.ds(s * width, width)] = low

    degree = (
        has_prev.astype(jnp.int32)
        + has_next.astype(jnp.int32)
        + has_below.astype(jnp.int32)
        + has_above.astype(jnp.int32)
    )
    pl.semaphore_wait(barrier, degree)

    def at(ref, k):
        return ref.at[pl.ds(k * CHUNK_ROWS, CHUNK_ROWS)]

    def state_copy(k):
        return pltpu.make_async_remote_copy(
            src_ref=at(out_ref, k), dst_ref=at(state, k), send_sem=state_send.at[k],
            recv_sem=state_recv.at[k], device_id=next_id, device_id_type=MESH,
        )

    def up_copy(k):
        return pltpu.make_async_remote_copy(
            src_ref=at(upward, k), dst_ref=at(from_below, k), send_sem=up_send.at[k],
            recv_sem=up_recv.at[k], device_id=above_id, device_id_type=MESH,
        )

    def down_copy(k):
        return pltpu.make_async_remote_copy(
            src_ref=at(downward, k), dst_ref=at(from_above, k), send_sem=down_send.at[k],
            recv_sem=down_recv.at[k], device_id=below_id, device_id_type=MESH,
        )

    def advance(k):
        @pl.when(has_prev)
        def _():
            state_copy(k).wait_recv()

        high, low = split(at(state, k)[...])

        def part(s):
            columns = pl.ds(s * width, width)
            return dot(high, map_high[:, columns]) + (
                dot(low, map_high[:, columns]) + dot(high, map_low[:, columns])
            )

        at(upward, k)[...] = part(2)

        @pl.when(has_above)
        def _():
            up_copy(k).start()

        at(downward, k)[...] = part(0)

        @pl.when(has_below)
        def _():
            down_copy(k).start()

        at(out_ref, k)[...] = part(1)

    def finish(k):
        @pl.when(has_below)
        def _():
            up_copy(k).wait_recv()
            at(out_ref, k)[...] += at(from_below, k)[...]

        @pl.when(has_above)
        def _():
            down_copy(k).wait_recv()
            at(out_ref, k)[...] += at(from_above, k)[...]

        @pl.when(has_next)
        def _():
            state_copy(k).start()

    for k in range(chunks + LAG):
        if k < chunks:
            advance(k)
        if k >= LAG:
            finish(k - LAG)

    for k in range(chunks):
        @pl.when(has_above)
        def _():
            up_copy(k).wait_send()

        @pl.when(has_below)
        def _():
            down_copy(k).wait_send()

        @pl.when(has_next)
        def _():
            state_copy(k).wait_send()


def local(sites, sectors, boundary, peps_row, sketch, charges, left_edge):
    _, width, phys, inner = boundary.shape
    depth = peps_row.shape[2]
    rows = left_edge.shape[0]
    chunks = rows // CHUNK_ROWS
    f32, bf16 = jnp.float32, jnp.bfloat16
    vmem = pl.BlockSpec(memory_space=pltpu.VMEM)
    hbm = pl.BlockSpec(memory_space=pl.ANY)
    dma = pltpu.SemaphoreType.DMA
    out = pl.pallas_call(
        functools.partial(kernel, sites, sectors, width, phys, depth),
        out_shape=jax.ShapeDtypeStruct((rows, width), f32),
        in_specs=[hbm, vmem, hbm, pl.BlockSpec(memory_space=pltpu.SMEM), vmem],
        out_specs=vmem,
        scratch_shapes=[
            pltpu.VMEM((width * phys, inner), bf16),
            pltpu.VMEM((width * depth, inner), bf16),
            pltpu.VMEM((depth, MAP_ROWS, inner), f32),
            pltpu.VMEM((depth, width, inner), bf16),
            pltpu.VMEM((width, 3 * inner), bf16),
            pltpu.VMEM((width, 3 * inner), bf16),
        ]
        + [pltpu.VMEM((rows, width), f32)] * 5
        + [dma((width // MAP_ROWS,)), dma(())]
        + [dma((chunks,))] * 6,
        compiler_params=pltpu.CompilerParams(collective_id=0, has_side_effects=True),
    )(
        boundary.reshape(width * phys, inner),
        peps_row[0].T,
        sketch.reshape(width * depth, inner),
        charges,
        left_edge,
    )
    return out[None]


def solution(mesh):
    in_specs = (
        P("site", "sector", None, None),
        P("site", None, None),
        P("site", "sector", None, None),
        P("site", None),
        P(None, "sector"),
    )
    out_specs = P("site", None, "sector")
    body = functools.partial(local, mesh.shape["site"], mesh.shape["sector"])
    return jax.shard_map(body, mesh=mesh, in_specs=in_specs, out_specs=out_specs, check_vma=False)
```

```python
import functools

import jax
import jax.numpy as jnp
from jax import lax
from jax.experimental import pallas as pl
from jax.experimental.pallas import tpu as pltpu
from jax.sharding import PartitionSpec as P

MESH = pl.DeviceIdType.MESH
CHUNK_ROWS = 64
LAG = 2
MAP_ROWS = 64
DOT_ROWS = 256
SPLIT_MID = False


def dot(a, b):
    return jnp.dot(a, b, preferred_element_type=jnp.float32)


def split(x):
    high = x.astype(jnp.bfloat16)
    low = (x - high.astype(jnp.float32)).astype(jnp.bfloat16)
    return high, low


def kernel(
    sites,
    sectors,
    width,
    phys,
    depth,
    boundary_ref,
    peps_ref,
    sketch_ref,
    charges_ref,
    left_ref,
    out_ref,
    boundary,
    sketch,
    absorbed,
    sorted_sketch,
    map_high,
    map_low,
    state,
    from_below,
    from_above,
    upward,
    downward,
    total,
    boundary_sem,
    sketch_sem,
    state_send,
    state_recv,
    up_send,
    up_recv,
    down_send,
    down_recv,
    result_sem,
):
    site = lax.axis_index("site")
    sector = lax.axis_index("sector")
    rows = left_ref.shape[0]
    chunks = rows // CHUNK_ROWS
    steps = width // MAP_ROWS
    f32, bf16 = jnp.float32, jnp.bfloat16

    sketch_copy = pltpu.make_async_copy(sketch_ref, sketch, sketch_sem)
    sketch_copy.start()
    slab = MAP_ROWS * phys
    slabs = []
    for i in range(steps):
        part = pl.ds(i * slab, slab)
        copy = pltpu.make_async_copy(boundary_ref.at[part], boundary.at[part], boundary_sem.at[i])
        copy.start()
        slabs.append(copy)

    barrier = pltpu.get_barrier_semaphore()
    has_prev, has_next = site > 0, site < sites - 1
    has_below, has_above = sector > 0, sector < sectors - 1

    def greet(condition, target):
        @pl.when(condition)
        def _():
            pl.semaphore_signal(barrier, inc=1, device_id=target, device_id_type=MESH)

    prev_id, next_id = (site - 1, sector), (site + 1, sector)
    below_id, above_id = (site, sector - 1), (site, sector + 1)
    greet(has_prev, prev_id)
    greet(has_next, next_id)
    greet(has_below, below_id)
    greet(has_above, above_id)

    @pl.when(site == 0)
    def _():
        state[...] = left_ref[...].astype(f32)

    @pl.when(jnp.logical_not(has_below))
    def _():
        from_below[...] = jnp.zeros_like(from_below)

    @pl.when(jnp.logical_not(has_above))
    def _():
        from_above[...] = jnp.zeros_like(from_above)

    group = width // phys
    size = group * depth
    iota = lambda shape, axis: lax.broadcasted_iota(jnp.int32, shape, axis)
    pick = (iota((size, depth), 0) // group == iota((size, depth), 1)).astype(f32).astype(bf16)
    tile = (iota((phys, width), 1) % phys == iota((phys, width), 0)).astype(f32).astype(bf16)
    by_row = dot(pick, peps_ref[...]).astype(bf16)
    same = iota((size, width), 0) % group == iota((size, width), 1) // phys
    spread = jnp.where(same, dot(by_row, tile), 0.0).astype(bf16)

    run = width // depth
    order = (
        iota((width, width), 1) == (iota((width, width), 0) % run) * depth + iota((width, width), 0) // run
    ).astype(f32).astype(bf16)
    sketch_copy.wait()
    for g in range(depth):
        moved = dot(order, sketch[pl.ds(g * width, width), :]).astype(bf16)
        for l in range(depth):
            sorted_sketch[l, pl.ds(g * run, run), :] = moved[l * run : (l + 1) * run]

    flags = [
        [(charges_ref[0, l] == s - 1).astype(f32) for l in range(depth)] for s in range(3)
    ]
    for i in range(steps):
        slabs[i].wait()
        for g in range(i * MAP_ROWS // group, (i + 1) * MAP_ROWS // group):
            grown = dot(spread, boundary[pl.ds(g * group * phys, width), :])
            for l in range(depth):
                absorbed[l, pl.ds(g * group, group), :] = grown[l * group : (l + 1) * group]
    for i in range(width // DOT_ROWS):
        part = pl.ds(i * DOT_ROWS, DOT_ROWS)
        sums = [None] * 3
        for l in range(depth):
            high, low = split(absorbed[l, part])
            both = dot(jnp.concatenate([high, low], axis=0), sorted_sketch[l])
            product = both[:DOT_ROWS] + both[DOT_ROWS:]
            for s in range(3):
                term = flags[s][l] * product
                sums[s] = term if sums[s] is None else sums[s] + term
        for s in range(3):
            high, low = split(sums[s])
            map_high[part, pl.ds(s * width, width)] = high
            map_low[part, pl.ds(s * width, width)] = low

    degree = (
        has_prev.astype(jnp.int32)
        + has_next.astype(jnp.int32)
        + has_below.astype(jnp.int32)
        + has_above.astype(jnp.int32)
    )
    pl.semaphore_wait(barrier, degree)

    def at(ref, k):
        return ref.at[pl.ds(k * CHUNK_ROWS, CHUNK_ROWS)]

    def state_copy(k):
        return pltpu.make_async_remote_copy(
            src_ref=at(total, k), dst_ref=at(state, k), send_sem=state_send.at[k],
            recv_sem=state_recv.at[k], device_id=next_id, device_id_type=MESH,
        )

    def result_copy(k):
        return pltpu.make_async_copy(at(total, k), at(out_ref, k), result_sem.at[k])

    def up_copy(k):
        return pltpu.make_async_remote_copy(
            src_ref=at(upward, k), dst_ref=at(from_below, k), send_sem=up_send.at[k],
            recv_sem=up_recv.at[k], device_id=above_id, device_id_type=MESH,
        )

    def down_copy(k):
        return pltpu.make_async_remote_copy(
            src_ref=at(downward, k), dst_ref=at(from_above, k), send_sem=down_send.at[k],
            recv_sem=down_recv.at[k], device_id=below_id, device_id_type=MESH,
        )

    def advance(k):
        @pl.when(has_prev)
        def _():
            state_copy(k).wait_recv()

        high, low = split(at(state, k)[...])
        both = jnp.concatenate([high, low], axis=0)

        def part(s):
            columns = pl.ds(s * width, width)
            twice = dot(both, map_high[:, columns])
            return twice[:CHUNK_ROWS] + (twice[CHUNK_ROWS:] + dot(high, map_low[:, columns]))

        at(upward, k)[...] = part(2)
        at(downward, k)[...] = part(0)
        if not SPLIT_MID:
            at(total, k)[...] = part(1)

        @pl.when(has_above)
        def _():
            up_copy(k).start()

        @pl.when(has_below)
        def _():
            down_copy(k).start()

        if SPLIT_MID:
            at(total, k)[...] = part(1)

    def finish(k):
        @pl.when(has_below)
        def _():
            up_copy(k).wait_recv()

        @pl.when(has_above)
        def _():
            down_copy(k).wait_recv()

        at(total, k)[...] += at(from_below, k)[...] + at(from_above, k)[...]

        @pl.when(has_next)
        def _():
            state_copy(k).start()

        result_copy(k).start()

    for k in range(chunks + LAG):
        if k < chunks:
            advance(k)
        if k >= LAG:
            finish(k - LAG)

    for k in range(chunks):
        result_copy(k).wait()

        @pl.when(has_above)
        def _():
            up_copy(k).wait_send()

        @pl.when(has_below)
        def _():
            down_copy(k).wait_send()

        @pl.when(has_next)
        def _():
            state_copy(k).wait_send()


def local(sites, sectors, boundary, peps_row, sketch, charges, left_edge):
    _, width, phys, inner = boundary.shape
    depth = peps_row.shape[2]
    rows = left_edge.shape[0]
    chunks = rows // CHUNK_ROWS
    f32, bf16 = jnp.float32, jnp.bfloat16
    vmem = pl.BlockSpec(memory_space=pltpu.VMEM)
    hbm = pl.BlockSpec(memory_space=pl.ANY)
    dma = pltpu.SemaphoreType.DMA
    out = pl.pallas_call(
        functools.partial(kernel, sites, sectors, width, phys, depth),
        out_shape=jax.ShapeDtypeStruct((rows, width), f32),
        in_specs=[hbm, vmem, hbm, pl.BlockSpec(memory_space=pltpu.SMEM), vmem],
        out_specs=hbm,
        scratch_shapes=[
            pltpu.VMEM((width * phys, inner), bf16),
            pltpu.VMEM((width * depth, inner), bf16),
            pltpu.VMEM((depth, width, inner), f32),
            pltpu.VMEM((depth, width, inner), bf16),
            pltpu.VMEM((width, 3 * inner), bf16),
            pltpu.VMEM((width, 3 * inner), bf16),
        ]
        + [pltpu.VMEM((rows, width), f32)] * 6
        + [dma((width // MAP_ROWS,)), dma(())]
        + [dma((chunks,))] * 7,
        compiler_params=pltpu.CompilerParams(collective_id=0, has_side_effects=True),
    )(
        boundary.reshape(width * phys, inner),
        peps_row[0].T,
        sketch.reshape(width * depth, inner),
        charges,
        left_edge,
    )
    return out[None]


def solution(mesh):
    in_specs = (
        P("site", "sector", None, None),
        P("site", None, None),
        P("site", "sector", None, None),
        P("site", None),
        P(None, "sector"),
    )
    out_specs = P("site", None, "sector")
    body = functools.partial(local, mesh.shape["site"], mesh.shape["sector"])
    return jax.shard_map(body, mesh=mesh, in_specs=in_specs, out_specs=out_specs, check_vma=False)
```

```python
import functools

import jax
import jax.numpy as jnp
from jax import lax
from jax.experimental import pallas as pl
from jax.experimental.pallas import tpu as pltpu
from jax.sharding import PartitionSpec as P

MESH = pl.DeviceIdType.MESH
CHUNK_ROWS = 32
LAG = 3
LAG_FIRST = 4
MAP_ROWS = 64
DOT_ROWS = 256
SPLIT_MID = False


def dot(a, b):
    return jnp.dot(a, b, preferred_element_type=jnp.float32)


def split(x):
    high = x.astype(jnp.bfloat16)
    low = (x - high.astype(jnp.float32)).astype(jnp.bfloat16)
    return high, low


def kernel(
    sites,
    sectors,
    width,
    phys,
    depth,
    boundary_ref,
    peps_ref,
    sketch_ref,
    charges_ref,
    left_ref,
    out_ref,
    boundary,
    sketch,
    absorbed,
    sorted_sketch,
    map_high,
    map_low,
    state,
    from_below,
    from_above,
    upward,
    downward,
    total,
    boundary_sem,
    sketch_sem,
    state_send,
    state_recv,
    up_send,
    up_recv,
    down_send,
    down_recv,
    result_sem,
):
    site = lax.axis_index("site")
    sector = lax.axis_index("sector")
    rows = left_ref.shape[0]
    chunks = rows // CHUNK_ROWS
    steps = width // MAP_ROWS
    f32, bf16 = jnp.float32, jnp.bfloat16

    sketch_copy = pltpu.make_async_copy(sketch_ref, sketch, sketch_sem)
    sketch_copy.start()
    slab = MAP_ROWS * phys
    slabs = []
    for i in range(steps):
        part = pl.ds(i * slab, slab)
        copy = pltpu.make_async_copy(boundary_ref.at[part], boundary.at[part], boundary_sem.at[i])
        copy.start()
        slabs.append(copy)

    barrier = pltpu.get_barrier_semaphore()
    has_prev, has_next = site > 0, site < sites - 1
    has_below, has_above = sector > 0, sector < sectors - 1

    def greet(condition, target):
        @pl.when(condition)
        def _():
            pl.semaphore_signal(barrier, inc=1, device_id=target, device_id_type=MESH)

    prev_id, next_id = (site - 1, sector), (site + 1, sector)
    below_id, above_id = (site, sector - 1), (site, sector + 1)
    greet(has_prev, prev_id)
    greet(has_next, next_id)
    greet(has_below, below_id)
    greet(has_above, above_id)

    @pl.when(site == 0)
    def _():
        state[...] = left_ref[...].astype(f32)

    @pl.when(jnp.logical_not(has_below))
    def _():
        from_below[...] = jnp.zeros_like(from_below)

    @pl.when(jnp.logical_not(has_above))
    def _():
        from_above[...] = jnp.zeros_like(from_above)

    group = width // phys
    size = group * depth
    iota = lambda shape, axis: lax.broadcasted_iota(jnp.int32, shape, axis)
    pick = (iota((size, depth), 0) // group == iota((size, depth), 1)).astype(f32).astype(bf16)
    tile = (iota((phys, width), 1) % phys == iota((phys, width), 0)).astype(f32).astype(bf16)
    by_row = dot(pick, peps_ref[...]).astype(bf16)
    same = iota((size, width), 0) % group == iota((size, width), 1) // phys
    spread = jnp.where(same, dot(by_row, tile), 0.0).astype(bf16)

    run = width // depth
    order = (
        iota((width, width), 1) == (iota((width, width), 0) % run) * depth + iota((width, width), 0) // run
    ).astype(f32).astype(bf16)
    sketch_copy.wait()
    for g in range(depth):
        moved = dot(order, sketch[pl.ds(g * width, width), :]).astype(bf16)
        for l in range(depth):
            sorted_sketch[l, pl.ds(g * run, run), :] = moved[l * run : (l + 1) * run]

    flags = [
        [(charges_ref[0, l] == s - 1).astype(f32) for l in range(depth)] for s in range(3)
    ]
    for i in range(steps):
        slabs[i].wait()
        for g in range(i * MAP_ROWS // group, (i + 1) * MAP_ROWS // group):
            grown = dot(spread, boundary[pl.ds(g * group * phys, width), :])
            for l in range(depth):
                absorbed[l, pl.ds(g * group, group), :] = grown[l * group : (l + 1) * group]
    for i in range(width // DOT_ROWS):
        part = pl.ds(i * DOT_ROWS, DOT_ROWS)
        sums = [None] * 3
        for l in range(depth):
            high, low = split(absorbed[l, part])
            both = dot(jnp.concatenate([high, low], axis=0), sorted_sketch[l])
            product = both[:DOT_ROWS] + both[DOT_ROWS:]
            for s in range(3):
                term = flags[s][l] * product
                sums[s] = term if sums[s] is None else sums[s] + term
        for s in range(3):
            high, low = split(sums[s])
            map_high[part, pl.ds(s * width, width)] = high
            map_low[part, pl.ds(s * width, width)] = low

    degree = (
        has_prev.astype(jnp.int32)
        + has_next.astype(jnp.int32)
        + has_below.astype(jnp.int32)
        + has_above.astype(jnp.int32)
    )
    pl.semaphore_wait(barrier, degree)

    def at(ref, k):
        return ref.at[pl.ds(k * CHUNK_ROWS, CHUNK_ROWS)]

    def state_copy(k):
        return pltpu.make_async_remote_copy(
            src_ref=at(total, k), dst_ref=at(state, k), send_sem=state_send.at[k],
            recv_sem=state_recv.at[k], device_id=next_id, device_id_type=MESH,
        )

    def result_copy(k):
        return pltpu.make_async_copy(at(total, k), at(out_ref, k), result_sem.at[k])

    def up_copy(k):
        return pltpu.make_async_remote_copy(
            src_ref=at(upward, k), dst_ref=at(from_below, k), send_sem=up_send.at[k],
            recv_sem=up_recv.at[k], device_id=above_id, device_id_type=MESH,
        )

    def down_copy(k):
        return pltpu.make_async_remote_copy(
            src_ref=at(downward, k), dst_ref=at(from_above, k), send_sem=down_send.at[k],
            recv_sem=down_recv.at[k], device_id=below_id, device_id_type=MESH,
        )

    def advance(k):
        @pl.when(has_prev)
        def _():
            state_copy(k).wait_recv()

        high, low = split(at(state, k)[...])
        both = jnp.concatenate([high, low], axis=0)

        def part(s):
            columns = pl.ds(s * width, width)
            twice = dot(both, map_high[:, columns])
            return twice[:CHUNK_ROWS] + (twice[CHUNK_ROWS:] + dot(high, map_low[:, columns]))

        at(upward, k)[...] = part(2)
        at(downward, k)[...] = part(0)
        if not SPLIT_MID:
            at(total, k)[...] = part(1)

        @pl.when(has_above)
        def _():
            up_copy(k).start()

        @pl.when(has_below)
        def _():
            down_copy(k).start()

        if SPLIT_MID:
            at(total, k)[...] = part(1)

    def finish(k):
        @pl.when(has_below)
        def _():
            up_copy(k).wait_recv()

        @pl.when(has_above)
        def _():
            down_copy(k).wait_recv()

        at(total, k)[...] += at(from_below, k)[...] + at(from_above, k)[...]

        @pl.when(has_next)
        def _():
            state_copy(k).start()

        result_copy(k).start()

    def stream(lag):
        for k in range(chunks + lag):
            if k < chunks:
                advance(k)
            if k >= lag:
                finish(k - lag)

    @pl.when(site == 0)
    def _():
        stream(LAG_FIRST)

    @pl.when(site > 0)
    def _():
        stream(LAG)

    for k in range(chunks):
        result_copy(k).wait()

        @pl.when(has_above)
        def _():
            up_copy(k).wait_send()

        @pl.when(has_below)
        def _():
            down_copy(k).wait_send()

        @pl.when(has_next)
        def _():
            state_copy(k).wait_send()


def local(sites, sectors, boundary, peps_row, sketch, charges, left_edge):
    _, width, phys, inner = boundary.shape
    depth = peps_row.shape[2]
    rows = left_edge.shape[0]
    chunks = rows // CHUNK_ROWS
    f32, bf16 = jnp.float32, jnp.bfloat16
    vmem = pl.BlockSpec(memory_space=pltpu.VMEM)
    hbm = pl.BlockSpec(memory_space=pl.ANY)
    dma = pltpu.SemaphoreType.DMA
    out = pl.pallas_call(
        functools.partial(kernel, sites, sectors, width, phys, depth),
        out_shape=jax.ShapeDtypeStruct((rows, width), f32),
        in_specs=[hbm, vmem, hbm, pl.BlockSpec(memory_space=pltpu.SMEM), vmem],
        out_specs=hbm,
        scratch_shapes=[
            pltpu.VMEM((width * phys, inner), bf16),
            pltpu.VMEM((width * depth, inner), bf16),
            pltpu.VMEM((depth, width, inner), f32),
            pltpu.VMEM((depth, width, inner), bf16),
            pltpu.VMEM((width, 3 * inner), bf16),
            pltpu.VMEM((width, 3 * inner), bf16),
        ]
        + [pltpu.VMEM((rows, width), f32)] * 6
        + [dma((width // MAP_ROWS,)), dma(())]
        + [dma((chunks,))] * 7,
        compiler_params=pltpu.CompilerParams(collective_id=0, has_side_effects=True),
    )(
        boundary.reshape(width * phys, inner),
        peps_row[0].T,
        sketch.reshape(width * depth, inner),
        charges,
        left_edge,
    )
    return out[None]


def solution(mesh):
    in_specs = (
        P("site", "sector", None, None),
        P("site", None, None),
        P("site", "sector", None, None),
        P("site", None),
        P(None, "sector"),
    )
    out_specs = P("site", None, "sector")
    body = functools.partial(local, mesh.shape["site"], mesh.shape["sector"])
    return jax.shard_map(body, mesh=mesh, in_specs=in_specs, out_specs=out_specs, check_vma=False)
```

```python
import functools

import jax
import jax.numpy as jnp
from jax import lax
from jax.experimental import pallas as pl
from jax.experimental.pallas import tpu as pltpu
from jax.sharding import PartitionSpec as P

MESH = pl.DeviceIdType.MESH
CHUNK_ROWS = 32
LAG = 3
LAG_FIRST = 4
MAP_ROWS = 64
DOT_ROWS = 256
SPLIT_MID = False


def dot(a, b):
    return jnp.dot(a, b, preferred_element_type=jnp.float32)


def split(x):
    high = x.astype(jnp.bfloat16)
    low = (x - high.astype(jnp.float32)).astype(jnp.bfloat16)
    return high, low


def kernel(
    sites,
    sectors,
    width,
    phys,
    depth,
    boundary_ref,
    peps_ref,
    sketch_ref,
    charges_ref,
    left_ref,
    out_ref,
    boundary,
    sketch,
    absorbed,
    sorted_sketch,
    map_high,
    map_low,
    state,
    from_below,
    from_above,
    upward,
    downward,
    total,
    boundary_sem,
    sketch_sem,
    state_send,
    state_recv,
    up_send,
    up_recv,
    down_send,
    down_recv,
    result_sem,
):
    site = lax.axis_index("site")
    sector = lax.axis_index("sector")
    rows = left_ref.shape[0]
    chunks = rows // CHUNK_ROWS
    steps = width // MAP_ROWS
    f32, bf16 = jnp.float32, jnp.bfloat16

    sketch_copy = pltpu.make_async_copy(sketch_ref, sketch, sketch_sem)
    sketch_copy.start()
    slab = MAP_ROWS * phys
    slabs = []
    for i in range(steps):
        part = pl.ds(i * slab, slab)
        copy = pltpu.make_async_copy(boundary_ref.at[part], boundary.at[part], boundary_sem.at[i])
        copy.start()
        slabs.append(copy)

    barrier = pltpu.get_barrier_semaphore()
    has_prev, has_next = site > 0, site < sites - 1
    has_below, has_above = sector > 0, sector < sectors - 1

    def greet(condition, target):
        @pl.when(condition)
        def _():
            pl.semaphore_signal(barrier, inc=1, device_id=target, device_id_type=MESH)

    prev_id, next_id = (site - 1, sector), (site + 1, sector)
    below_id, above_id = (site, sector - 1), (site, sector + 1)
    greet(has_prev, prev_id)
    greet(has_next, next_id)
    greet(has_below, below_id)
    greet(has_above, above_id)

    @pl.when(site == 0)
    def _():
        state[...] = left_ref[...].astype(f32)

    @pl.when(jnp.logical_not(has_below))
    def _():
        from_below[...] = jnp.zeros_like(from_below)

    @pl.when(jnp.logical_not(has_above))
    def _():
        from_above[...] = jnp.zeros_like(from_above)

    group = width // phys
    size = group * depth
    iota = lambda shape, axis: lax.broadcasted_iota(jnp.int32, shape, axis)
    pick = (iota((size, depth), 0) // group == iota((size, depth), 1)).astype(f32).astype(bf16)
    tile = (iota((phys, width), 1) % phys == iota((phys, width), 0)).astype(f32).astype(bf16)
    by_row = dot(pick, peps_ref[...]).astype(bf16)
    same = iota((size, width), 0) % group == iota((size, width), 1) // phys
    spread = jnp.where(same, dot(by_row, tile), 0.0).astype(bf16)

    run = width // depth
    order = (
        iota((width, width), 1) == (iota((width, width), 0) % run) * depth + iota((width, width), 0) // run
    ).astype(f32).astype(bf16)
    sketch_copy.wait()
    for g in range(depth):
        moved = dot(order, sketch[pl.ds(g * width, width), :]).astype(bf16)
        for l in range(depth):
            sorted_sketch[l, pl.ds(g * run, run), :] = moved[l * run : (l + 1) * run]

    flags = [
        [(charges_ref[0, l] == s - 1).astype(f32) for l in range(depth)] for s in range(3)
    ]
    for i in range(steps):
        slabs[i].wait()
        for g in range(i * MAP_ROWS // group, (i + 1) * MAP_ROWS // group):
            grown = dot(spread, boundary[pl.ds(g * group * phys, width), :])
            for l in range(depth):
                absorbed[l, pl.ds(g * group, group), :] = grown[l * group : (l + 1) * group]
    for i in range(width // DOT_ROWS):
        part = pl.ds(i * DOT_ROWS, DOT_ROWS)
        sums = [None] * 3
        for l in range(depth):
            high, low = split(absorbed[l, part])
            both = dot(jnp.concatenate([high, low], axis=0), sorted_sketch[l])
            product = both[:DOT_ROWS] + both[DOT_ROWS:]
            for s in range(3):
                term = flags[s][l] * product
                sums[s] = term if sums[s] is None else sums[s] + term
        for s in range(3):
            high, low = split(sums[s])
            map_high[part, pl.ds(s * width, width)] = high
            map_low[part, pl.ds(s * width, width)] = low

    degree = (
        has_prev.astype(jnp.int32)
        + has_next.astype(jnp.int32)
        + has_below.astype(jnp.int32)
        + has_above.astype(jnp.int32)
    )
    pl.semaphore_wait(barrier, degree)

    def at(ref, k):
        return ref.at[pl.ds(k * CHUNK_ROWS, CHUNK_ROWS)]

    def state_copy(k):
        return pltpu.make_async_remote_copy(
            src_ref=at(total, k), dst_ref=at(state, k), send_sem=state_send.at[k],
            recv_sem=state_recv.at[k], device_id=next_id, device_id_type=MESH,
        )

    def result_copy(k):
        return pltpu.make_async_copy(at(total, k), at(out_ref, k), result_sem.at[k])

    def up_copy(k):
        return pltpu.make_async_remote_copy(
            src_ref=at(upward, k), dst_ref=at(from_below, k), send_sem=up_send.at[k],
            recv_sem=up_recv.at[k], device_id=above_id, device_id_type=MESH,
        )

    def down_copy(k):
        return pltpu.make_async_remote_copy(
            src_ref=at(downward, k), dst_ref=at(from_above, k), send_sem=down_send.at[k],
            recv_sem=down_recv.at[k], device_id=below_id, device_id_type=MESH,
        )

    def advance(k):
        @pl.when(has_prev)
        def _():
            state_copy(k).wait_recv()

        high, low = split(at(state, k)[...])
        both = jnp.concatenate([high, low], axis=0)

        twice = dot(both, map_high[...])
        wide = twice[:CHUNK_ROWS] + (twice[CHUNK_ROWS:] + dot(high, map_low[...]))

        def part(s):
            return wide[:, s * width : (s + 1) * width]

        at(upward, k)[...] = part(2)
        at(downward, k)[...] = part(0)
        if not SPLIT_MID:
            at(total, k)[...] = part(1)

        @pl.when(has_above)
        def _():
            up_copy(k).start()

        @pl.when(has_below)
        def _():
            down_copy(k).start()

        if SPLIT_MID:
            at(total, k)[...] = part(1)

    def finish(k):
        @pl.when(has_below)
        def _():
            up_copy(k).wait_recv()

        @pl.when(has_above)
        def _():
            down_copy(k).wait_recv()

        at(total, k)[...] += at(from_below, k)[...] + at(from_above, k)[...]

        @pl.when(has_next)
        def _():
            state_copy(k).start()

        result_copy(k).start()

    def stream(lag):
        for k in range(chunks + lag):
            if k < chunks:
                advance(k)
            if k >= lag:
                finish(k - lag)

    @pl.when(site == 0)
    def _():
        stream(LAG_FIRST)

    @pl.when(site > 0)
    def _():
        stream(LAG)

    for k in range(chunks):
        result_copy(k).wait()

        @pl.when(has_above)
        def _():
            up_copy(k).wait_send()

        @pl.when(has_below)
        def _():
            down_copy(k).wait_send()

        @pl.when(has_next)
        def _():
            state_copy(k).wait_send()


def local(sites, sectors, boundary, peps_row, sketch, charges, left_edge):
    _, width, phys, inner = boundary.shape
    depth = peps_row.shape[2]
    rows = left_edge.shape[0]
    chunks = rows // CHUNK_ROWS
    f32, bf16 = jnp.float32, jnp.bfloat16
    vmem = pl.BlockSpec(memory_space=pltpu.VMEM)
    hbm = pl.BlockSpec(memory_space=pl.ANY)
    dma = pltpu.SemaphoreType.DMA
    out = pl.pallas_call(
        functools.partial(kernel, sites, sectors, width, phys, depth),
        out_shape=jax.ShapeDtypeStruct((rows, width), f32),
        in_specs=[hbm, vmem, hbm, pl.BlockSpec(memory_space=pltpu.SMEM), vmem],
        out_specs=hbm,
        scratch_shapes=[
            pltpu.VMEM((width * phys, inner), bf16),
            pltpu.VMEM((width * depth, inner), bf16),
            pltpu.VMEM((depth, width, inner), f32),
            pltpu.VMEM((depth, width, inner), bf16),
            pltpu.VMEM((width, 3 * inner), bf16),
            pltpu.VMEM((width, 3 * inner), bf16),
        ]
        + [pltpu.VMEM((rows, width), f32)] * 6
        + [dma((width // MAP_ROWS,)), dma(())]
        + [dma((chunks,))] * 7,
        compiler_params=pltpu.CompilerParams(collective_id=0, has_side_effects=True),
    )(
        boundary.reshape(width * phys, inner),
        peps_row[0].T,
        sketch.reshape(width * depth, inner),
        charges,
        left_edge,
    )
    return out[None]


def solution(mesh):
    in_specs = (
        P("site", "sector", None, None),
        P("site", None, None),
        P("site", "sector", None, None),
        P("site", None),
        P(None, "sector"),
    )
    out_specs = P("site", None, "sector")
    body = functools.partial(local, mesh.shape["site"], mesh.shape["sector"])
    return jax.shard_map(body, mesh=mesh, in_specs=in_specs, out_specs=out_specs, check_vma=False)
```
